256 devices in a mesh: row: 8 (over z_lo, core), col: 32 (over z_hi, x, y).
Axes of the slice: x: 4, y: 4, z: 8 (z_hi: 2, z_lo: 4; z = z_hi * 4 + z_lo), core: 2. Of those that a mesh axis runs over, the one named last changes fastest.
Arguments:
- spectra: bfloat16 [2, 512, 20480], P(None, None, ('row', 'col')), may hold values from -6 to 6
Outputs:
- cross: bfloat16 [2, 20480, 20480], P(None, 'row', 'col')
The draws below stay inside these ranges and needn't reach their ends.
All inputs are finite; a program needn't handle non-finite values.
Results may differ from the reference program's by a relative error of at most 0.0049.
Values may be sent and summed in bfloat16 or wider, within the bound.
No kernel may reach another device: no remote copies, remote signals or barrier semaphores. Data moves between devices by JAX's collectives and lax.ppermute only.
A program may use at most 128 MiB of HBM per device.

```python
import jax
import jax.numpy as jnp
from jax import lax

C = 20480
SEG = 512
N_ROW = 8


def block_scale(own_key, dims, shards, low, largest):
    gain = 1.0
    for position, parts in shards:
        steps = jax.random.uniform(jax.random.fold_in(jax.random.fold_in(own_key, 6), position), (parts,), jnp.float32, low / len(shards), largest / len(shards))
        gain = gain * jnp.repeat(jnp.exp(steps), dims[position] // parts).reshape((-1,) + (1,) * (len(dims) - 1 - position))
    return gain


def bell_draw(stream_key, dims, spread, reach, pieces=(), dtype=jnp.bfloat16):
    values = jax.random.normal(stream_key, dims, jnp.float32) * spread
    if len(pieces) > 0:
        values = block_scale(stream_key, dims, pieces, -0.22, 0.18) * values
    return jnp.clip(values, min=-reach, max=reach).astype(dtype)


def setup_inputs(seed: int = 0) -> dict:
    streams_of = jax.random.split(jax.random.key(seed), 2)
    spectra = bell_draw(streams_of[0], (2, SEG, C), 1.0, 6.0, ((2, 256),))
    return {"spectra": spectra}


def whiten(spectra):
    floats = spectra.astype(jnp.float32)
    magnitude = jnp.sqrt(floats[0] * floats[0] + floats[1] * floats[1])
    return (floats / jnp.maximum(magnitude, 1.0)).astype(jnp.bfloat16)

def reference(spectra):
    whitened = whiten(spectra).astype(jnp.float32)
    row_width = C // N_ROW
    stacked = jnp.moveaxis(whitened.reshape(2, SEG, N_ROW, row_width), 2, 0)
    highest = lax.Precision.HIGHEST

    def row_cross(row_block):
        real_part = jnp.dot(row_block[0].T, whitened[0], precision=highest) + jnp.dot(row_block[1].T, whitened[1], precision=highest)
        imag_part = jnp.dot(row_block[1].T, whitened[0], precision=highest) - jnp.dot(row_block[0].T, whitened[1], precision=highest)
        return (jnp.stack([real_part, imag_part]) / SEG).astype(jnp.bfloat16)
    results = lax.map(row_cross, stacked)
    return jnp.moveaxis(results, 0, 1).reshape(2, C, C)
```

```python
import functools
import itertools

import jax
import jax.numpy as jnp
from jax import lax
from jax.experimental import pallas as pl
from jax.experimental.pallas import tpu as pltpu
from jax.sharding import Mesh, PartitionSpec as P


AXES = ("zl", "core", "zh", "x", "y")
SIZES = (4, 2, 2, 4, 4)
NT = (((1,), (1,)), ((), ()))


def linear(place):
    index = 0
    for coordinate, size in zip(place, SIZES):
        index = index * size + coordinate
    return index


def permute(value, name, target):
    pairs = [(linear(p), linear(target(*p))) for p in itertools.product(*map(range, SIZES))]
    with jax.named_scope(name):
        return lax.ppermute(value, AXES, pairs)


def first_shift(step):
    def target(zl, core, zh, x, y):
        return (zl, core, zh, (x + step) % 4, y) if core == 0 else (zl, core, zh, x, (y + step) % 4)
    return target


def second_shift(step):
    def target(zl, core, zh, x, y):
        return (zl, core, zh, x, (y + step) % 4) if core == 0 else (zl, core, zh, (x + step) % 4, y)
    return target


def across(zl, core, zh, x, y):
    return (zl, core, 1 - zh, x, y)


def to_panel(zl, core, zh, x, y):
    block = linear((zl, core, zh, x, y))
    column, slot = block // 8, block % 8
    return (slot % 4, slot // 4, column // 16, column // 4 % 4, column % 4)


def line_shift(step):
    return lambda zl, core, zh, x, y: ((zl + step) % 4, core, zh, x, y)


def other_core(zl, core, zh, x, y):
    return (zl, 1 - core, zh, x, y)


def whiten_kernel(spectra, whitened):
    real = spectra[0].astype(jnp.float32)
    imag = spectra[1].astype(jnp.float32)
    divisor = jnp.maximum(jnp.sqrt(real * real + imag * imag), 1.0)
    whitened[0] = (real / divisor).astype(jnp.bfloat16)
    whitened[1] = (imag / divisor).astype(jnp.bfloat16)


def whiten(spectra):
    return pl.pallas_call(
        whiten_kernel,
        out_shape=jax.ShapeDtypeStruct(spectra.shape, jnp.bfloat16),
        name="whiten",
    )(spectra)


def gather_plane(share, tag):
    back = permute(share, tag + "p1a", first_shift(1))
    ahead = permute(share, tag + "p1b", first_shift(-1))
    far = permute(share, tag + "p1c", first_shift(2))
    line = jnp.stack([share, back, ahead, far])
    line_back = permute(line, tag + "p2a", second_shift(1))
    line_ahead = permute(line, tag + "p2b", second_shift(-1))
    far_low = permute(line_back[:2], tag + "p3a", second_shift(1))
    far_high = permute(line_ahead[2:], tag + "p3b", second_shift(-1))
    return [line, line_back, line_ahead, jnp.concatenate([far_low, far_high])]


def share_places(zh, x, y, core):
    places = []
    for second in (0, -1, 1, 2):
        for first in (0, -1, 1, 2):
            px = jnp.where(core == 0, x + first, x + second) % 4
            py = jnp.where(core == 0, y + second, y + first) % 4
            places.append(zh * 16 + px * 4 + py)
    return places


def product_kernel(scale, width, places, order, near, other, *refs):
    count = len(refs) - 4
    groups, (out, panel, tile, sem) = refs[:count], refs[count:]
    for core in range(2):
        for j in range(4):
            slot = order[core * 4 + j]
            at = (core * 4 + j) * width

            @pl.when(order[8] == core)
            def _():
                panel[:, at:at + width] = near[slot]

            @pl.when(order[8] != core)
            def _():
                panel[:, at:at + width] = other[slot]
    def copies(g):
        return [
            pltpu.make_async_copy(
                tile.at[g % 2, :, pl.ds(s * width, width)],
                out.at[:, pl.ds(pl.multiple_of(places[g * 4 + s] * width, 16), width)],
                sem.at[g % 2],
            )
            for s in range(4)
        ]
    for g in range(count):
        real = groups[g][:, 0].reshape(4 * width, -1)
        imag = groups[g][:, 1].reshape(4 * width, -1)
        def dot(a, b):
            return lax.dot_general(a, b, NT, preferred_element_type=jnp.float32)
        if g >= 2:
            for copy in copies(g - 2):
                copy.wait()
        tile[g % 2, 0] = ((dot(real, panel[0]) + dot(imag, panel[1])) * scale).astype(jnp.bfloat16)
        tile[g % 2, 1] = ((dot(imag, panel[0]) - dot(real, panel[1])) * scale).astype(jnp.bfloat16)
        for copy in copies(g):
            copy.start()
    for g in range(max(count - 2, 0), count):
        for copy in copies(g):
            copy.wait()


def per_device(spectra):
    spectra = jnp.transpose(spectra, (0, 2, 1))
    width, segments = spectra.shape[1:]
    zl, core, zh, x, y = (lax.axis_index(a) for a in AXES)
    own = whiten(spectra)
    crossed = permute(own, "zx", across)
    piece = permute(own, "panel", to_panel)
    near = jnp.stack([piece] + [permute(piece, "line%d" % s, line_shift(s)) for s in (1, 2, 3)])
    other = permute(near, "cores", other_core)
    groups = gather_plane(own, "o") + gather_plane(crossed, "q")
    places = jnp.stack(share_places(zh, x, y, core) + share_places(1 - zh, x, y, core)).astype(jnp.int32)
    order = jnp.stack([(zl - j) % 4 for j in range(4)] * 2 + [core]).astype(jnp.int32)
    vmem = pl.BlockSpec(memory_space=pltpu.VMEM)
    smem = pl.BlockSpec(memory_space=pltpu.SMEM)
    channels = width * 32
    panel = width * 8
    return pl.pallas_call(
        functools.partial(product_kernel, 1.0 / segments, width),
        in_specs=[smem, smem] + [vmem] * (2 + len(groups)),
        out_specs=pl.BlockSpec(memory_space=pl.ANY),
        out_shape=jax.ShapeDtypeStruct((2, channels, panel), jnp.bfloat16),
        scratch_shapes=[
            pltpu.VMEM((2, panel, segments), jnp.bfloat16),
            pltpu.VMEM((2, 2, 4 * width, panel), jnp.bfloat16),
            pltpu.SemaphoreType.DMA((2,)),
        ],
        compiler_params=pltpu.CompilerParams(vmem_limit_bytes=32 << 20),
        name="product",
    )(places, order, near, other, *groups)


def solution(mesh):
    fine = Mesh(mesh.devices.reshape(SIZES), AXES)
    return jax.shard_map(
        per_device,
        mesh=fine,
        in_specs=(P(None, None, AXES),),
        out_specs=P(None, ("zl", "core"), ("zh", "x", "y")),
        check_vma=False,
    )
```

```python
import functools
import itertools

import jax
import jax.numpy as jnp
from jax import lax
from jax.experimental import pallas as pl
from jax.experimental.pallas import tpu as pltpu
from jax.sharding import Mesh, PartitionSpec as P


AXES = ("zl", "core", "zh", "x", "y")
SIZES = (4, 2, 2, 4, 4)
NT = (((1,), (1,)), ((), ()))
STEPS = (0, -1, 1, 2)
VMEM = pl.BlockSpec(memory_space=pltpu.VMEM)
ANY = pl.BlockSpec(memory_space=pl.ANY)


def linear(place):
    index = 0
    for coordinate, size in zip(place, SIZES):
        index = index * size + coordinate
    return index


def permute(value, target):
    pairs = [(linear(p), linear(target(*p))) for p in itertools.product(*map(range, SIZES))]
    return lax.ppermute(value, AXES, pairs)


def first_shift(step):
    def target(zl, core, zh, x, y):
        return (zl, core, zh, (x + step) % 4, y) if core == 0 else (zl, core, zh, x, (y + step) % 4)

    return target


def second_shift(step):
    def target(zl, core, zh, x, y):
        return (zl, core, zh, x, (y + step) % 4) if core == 0 else (zl, core, zh, (x + step) % 4, y)

    return target


def across(zl, core, zh, x, y):
    return (zl, core, 1 - zh, x, y)


def to_panel(zl, core, zh, x, y):
    block = linear((zl, core, zh, x, y))
    column, slot = block // 8, block % 8
    return (slot % 4, slot // 4, column // 16, column // 4 % 4, column % 4)


def line_swap(bits):
    return lambda zl, core, zh, x, y: (zl ^ bits, core, zh, x, y)


def other_core(zl, core, zh, x, y):
    return (zl, 1 - core, zh, x, y)


def whiten_kernel(spectra, whitened):
    real = spectra[0].astype(jnp.float32)
    imag = spectra[1].astype(jnp.float32)
    factor = jnp.minimum(lax.rsqrt(real * real + imag * imag), 1.0)
    whitened[0] = (real * factor).astype(jnp.bfloat16)
    whitened[1] = (imag * factor).astype(jnp.bfloat16)


def whiten(spectra):
    return pl.pallas_call(
        whiten_kernel,
        out_shape=jax.ShapeDtypeStruct(spectra.shape, jnp.bfloat16),
        compiler_params=pltpu.CompilerParams(vmem_limit_bytes=4 << 20),
        name="whiten",
    )(spectra)


def stack_kernel(*refs):
    *shares, line = refs
    for s, share in enumerate(shares):
        line[s] = share[...]


def stack(shares):
    return pl.pallas_call(
        stack_kernel,
        in_specs=[VMEM] * len(shares),
        out_specs=VMEM,
        out_shape=jax.ShapeDtypeStruct((len(shares),) + shares[0].shape, shares[0].dtype),
        compiler_params=pltpu.CompilerParams(vmem_limit_bytes=4 << 20),
        name="stack",
    )(*shares)


def product_kernel(scale, width, lines, *refs):
    count = len(lines)
    pieces, groups = refs[:8], refs[8:8 + count]
    out, panel, tile, sem = refs[-4:]
    zl, core, zh, x, y = (lax.axis_index(a) for a in AXES)
    for s, piece in enumerate(pieces):
        slot = (core ^ (s // 4)) * 4 + (zl ^ (s % 4))
        panel[:, pl.ds(pl.multiple_of(slot * width, 16), width), :] = piece[...]

    def row(g, s):
        plane, second = lines[g]
        first = STEPS[s]
        px = (x + jnp.where(core == 0, first, second) + 4) % 4
        py = (y + jnp.where(core == 0, second, first) + 4) % 4
        return pl.multiple_of(((zh ^ plane) * 16 + px * 4 + py) * width, 16)

    def copies(g):
        return [
            pltpu.make_async_copy(
                tile.at[g % 2, :, pl.ds(s * width, width)],
                out.at[:, pl.ds(row(g, s), width)],
                sem.at[g % 2],
            )
            for s in range(4)
        ]

    def dot(a, b):
        return lax.dot_general(a, b, NT, preferred_element_type=jnp.float32)

    for g in range(count):
        real = groups[g][:, 0].reshape(4 * width, -1)
        imag = groups[g][:, 1].reshape(4 * width, -1)
        if g >= 2:
            for copy in copies(g - 2):
                copy.wait()
        tile[g % 2, 0] = ((dot(real, panel[0]) + dot(imag, panel[1])) * scale).astype(jnp.bfloat16)
        tile[g % 2, 1] = ((dot(imag, panel[0]) - dot(real, panel[1])) * scale).astype(jnp.bfloat16)
        for copy in copies(g):
            copy.start()
    for g in range(max(count - 2, 0), count):
        for copy in copies(g):
            copy.wait()


def product(out, shape, pieces, groups, lines):
    count, width, segments = len(groups), groups[0].shape[2], groups[0].shape[3]
    kept = [] if out is None else [out]
    return pl.pallas_call(
        functools.partial(product_kernel, 1.0 / segments, width, lines),
        in_specs=[VMEM] * (8 + count) + [ANY] * len(kept),
        out_specs=ANY,
        out_shape=jax.ShapeDtypeStruct(shape, jnp.bfloat16),
        input_output_aliases={8 + count: 0} if kept else {},
        scratch_shapes=[
            pltpu.VMEM((2, shape[2], segments), jnp.bfloat16),
            pltpu.VMEM((2, 2, 4 * width, shape[2]), jnp.bfloat16),
            pltpu.SemaphoreType.DMA((2,)),
        ],
        cost_estimate=pl.CostEstimate(
            flops=count * 32 * width * shape[2] * segments, bytes_accessed=1 << 20, transcendentals=0
        ),
        compiler_params=pltpu.CompilerParams(vmem_limit_bytes=12 << 20),
    )(*pieces, *groups, *kept)


def per_device(spectra):
    spectra = jnp.transpose(spectra, (0, 2, 1))
    width, _ = spectra.shape[1:]
    own = whiten(spectra)
    piece = permute(own, to_panel)
    crossed = permute(own, across)

    def line(share):
        back = permute(share, first_shift(1))
        ahead = permute(share, first_shift(-1))
        far = permute(share, first_shift(2))
        return stack([share, back, ahead, far])

    o0 = line(own)
    o_back = permute(o0, second_shift(1))
    o_ahead = permute(o0, second_shift(-1))
    o_far = permute(o_back, second_shift(1))
    q0 = line(crossed)
    q_back = permute(q0, second_shift(1))
    q_ahead = permute(q0, second_shift(-1))
    q_far = permute(q_ahead, second_shift(-1))

    near1 = permute(piece, line_swap(1))
    near2 = permute(piece, line_swap(2))
    near3 = permute(near2, line_swap(1))
    near = [piece, near1, near2, near3]
    other = [permute(n, other_core) for n in near]
    pieces = near + other
    shape = (2, 32 * width, 8 * width)
    out = product(
        None, shape, pieces,
        [o0, o_back, o_ahead, q0, q_back, q_ahead],
        [(0, 0), (0, -1), (0, 1), (1, 0), (1, -1), (1, 1)],
    )
    return product(out, shape, pieces, [o_far, q_far], [(0, 2), (1, 2)])


def solution(mesh):
    fine = Mesh(mesh.devices.reshape(SIZES), AXES)
    return jax.shard_map(
        per_device,
        mesh=fine,
        in_specs=(P(None, None, AXES),),
        out_specs=P(None, ("zl", "core"), ("zh", "x", "y")),
        check_vma=False,
    )
```

```python
import functools
import itertools

import jax
import jax.numpy as jnp
from jax import lax
from jax.experimental import pallas as pl
from jax.experimental.pallas import tpu as pltpu
from jax.sharding import Mesh, PartitionSpec as P


AXES = ("zl", "core", "zh", "x", "y")
SIZES = (4, 2, 2, 4, 4)
NT = (((1,), (1,)), ((), ()))
STEPS = (0, -1, 1, 2)
VMEM = pl.BlockSpec(memory_space=pltpu.VMEM)
ANY = pl.BlockSpec(memory_space=pl.ANY)


def linear(place):
    index = 0
    for coordinate, size in zip(place, SIZES):
        index = index * size + coordinate
    return index


def permute(value, target):
    pairs = [(linear(p), linear(target(*p))) for p in itertools.product(*map(range, SIZES))]
    return lax.ppermute(value, AXES, pairs)


def first_shift(step):
    def target(zl, core, zh, x, y):
        return (zl, core, zh, (x + step) % 4, y) if core == 0 else (zl, core, zh, x, (y + step) % 4)

    return target


def second_shift(step):
    def target(zl, core, zh, x, y):
        return (zl, core, zh, x, (y + step) % 4) if core == 0 else (zl, core, zh, (x + step) % 4, y)

    return target


def across(zl, core, zh, x, y):
    return (zl, core, 1 - zh, x, y)


def to_panel(zl, core, zh, x, y):
    block = linear((zl, core, zh, x, y))
    column, slot = block // 8, block % 8
    return (slot % 4, slot // 4, column // 16, column // 4 % 4, column % 4)


def line_swap(bits):
    return lambda zl, core, zh, x, y: (zl ^ bits, core, zh, x, y)


def other_core(zl, core, zh, x, y):
    return (zl, 1 - core, zh, x, y)


def whiten_kernel(spectra, whitened):
    real = spectra[0].astype(jnp.float32)
    imag = spectra[1].astype(jnp.float32)
    factor = jnp.minimum(lax.rsqrt(real * real + imag * imag), 1.0)
    whitened[0] = (real * factor).astype(jnp.bfloat16)
    whitened[1] = (imag * factor).astype(jnp.bfloat16)


def whiten(spectra):
    return pl.pallas_call(
        whiten_kernel,
        out_shape=jax.ShapeDtypeStruct(spectra.shape, jnp.bfloat16),
        compiler_params=pltpu.CompilerParams(vmem_limit_bytes=4 << 20),
        name="whiten",
    )(spectra)


def stack_kernel(*refs):
    *shares, line = refs
    for s, share in enumerate(shares):
        line[s] = share[...]


def stack(shares):
    return pl.pallas_call(
        stack_kernel,
        in_specs=[VMEM] * len(shares),
        out_specs=VMEM,
        out_shape=jax.ShapeDtypeStruct((len(shares),) + shares[0].shape, shares[0].dtype),
        compiler_params=pltpu.CompilerParams(vmem_limit_bytes=4 << 20),
        name="stack",
    )(*shares)


def row_of(width, line, s):
    _, core, zh, x, y = (lax.axis_index(a) for a in AXES)
    plane, second = line
    px = (x + jnp.where(core == 0, STEPS[s], second) + 4) % 4
    py = (y + jnp.where(core == 0, second, STEPS[s]) + 4) % 4
    return pl.multiple_of(((zh ^ plane) * 16 + px * 4 + py) * width, 16)


def multiply(scale, width, lines, groups, panel, out, tile, sem):
    pairs = [range(g, min(g + 2, len(groups))) for g in range(0, len(groups), 2)]

    def copies(n):
        return [
            pltpu.make_async_copy(
                tile.at[n % 2, :, pl.ds((k * 4 + s) * width, width)],
                out.at[:, pl.ds(row_of(width, lines[g], s), width)],
                sem.at[n % 2],
            )
            for k, g in enumerate(pairs[n])
            for s in range(4)
        ]

    def dot(a, b):
        return lax.dot_general(a, b, NT, preferred_element_type=jnp.float32)

    for n, pair in enumerate(pairs):
        rows = len(pair) * 4 * width
        parts = [jnp.concatenate([groups[g][:, k].reshape(4 * width, -1) for g in pair]) for k in range(2)]
        left = jnp.concatenate(parts, 1)
        if n >= 2:
            for copy in copies(n - 2):
                copy.wait()
        real = dot(left, jnp.concatenate([panel[0], panel[1]], 1))
        tile[n % 2, 0, :rows] = (real * scale).astype(jnp.bfloat16)
        imag = dot(left, jnp.concatenate([panel[2], panel[0]], 1))
        tile[n % 2, 1, :rows] = (imag * scale).astype(jnp.bfloat16)
        for copy in copies(n):
            copy.start()
    for n in range(max(len(pairs) - 2, 0), len(pairs)):
        for copy in copies(n):
            copy.wait()


def first_kernel(scale, width, lines, *refs):
    pieces, groups = refs[:8], refs[8:8 + len(lines)]
    out, panel, tile, sem = refs[-4:]
    zl, core = lax.axis_index("zl"), lax.axis_index("core")
    for s, piece in enumerate(pieces):
        slot = (core ^ (s // 4)) * 4 + (zl ^ (s % 4))
        at = pl.ds(pl.multiple_of(slot * width, 16), width)
        panel[0, at, :] = piece[0]
        panel[1, at, :] = piece[1]
        panel[2, at, :] = -piece[1]
    multiply(scale, width, lines, groups, panel, out, tile, sem)


def rest_kernel(scale, width, lines, panel, *refs):
    groups = refs[:len(lines)]
    out, tile, sem = refs[-3:]
    multiply(scale, width, lines, groups, panel, out, tile, sem)


def options(count, width, columns, segments):
    return dict(
        scratch_shapes=[
            pltpu.VMEM((2, 2, min(count, 2) * 4 * width, columns), jnp.bfloat16),
            pltpu.SemaphoreType.DMA((2,)),
        ],
        cost_estimate=pl.CostEstimate(
            flops=count * 32 * width * columns * segments, bytes_accessed=1 << 20, transcendentals=0
        ),
        compiler_params=pltpu.CompilerParams(vmem_limit_bytes=20 << 20),
    )


def first_product(pieces, groups, lines):
    count, (_, _, width, segments) = len(groups), groups[0].shape
    return pl.pallas_call(
        functools.partial(first_kernel, 1.0 / segments, width, lines),
        in_specs=[VMEM] * (8 + count),
        out_specs=[ANY, VMEM],
        out_shape=[
            jax.ShapeDtypeStruct((2, 32 * width, 8 * width), jnp.bfloat16),
            jax.ShapeDtypeStruct((3, 8 * width, segments), jnp.bfloat16),
        ],
        **options(count, width, 8 * width, segments),
    )(*pieces, *groups)


def rest_product(out, panel, groups, lines):
    count, (_, _, width, segments) = len(groups), groups[0].shape
    return pl.pallas_call(
        functools.partial(rest_kernel, 1.0 / segments, width, lines),
        in_specs=[VMEM] * (1 + count) + [ANY],
        out_specs=ANY,
        out_shape=jax.ShapeDtypeStruct(out.shape, jnp.bfloat16),
        input_output_aliases={1 + count: 0},
        **options(count, width, 8 * width, segments),
    )(panel, *groups, out)


def per_device(spectra):
    spectra = jnp.transpose(spectra, (0, 2, 1))
    own = whiten(spectra)
    piece = permute(own, to_panel)
    crossed = whiten(permute(spectra, across))

    def line(share):
        back = permute(share, first_shift(1))
        ahead = permute(share, first_shift(-1))
        far = permute(share, first_shift(2))
        return stack([share, back, ahead, far])

    o0 = line(own)
    o_back = permute(o0, second_shift(1))
    o_ahead = permute(o0, second_shift(-1))
    o_far = permute(o_back, second_shift(1))
    q0 = line(crossed)
    q_back = permute(q0, second_shift(1))
    q_ahead = permute(q0, second_shift(-1))
    q_far = permute(q_ahead, second_shift(-1))

    near1 = permute(piece, line_swap(1))
    near2 = permute(piece, line_swap(2))
    near3 = permute(near2, line_swap(1))
    near = [piece, near1, near2, near3]
    other = [permute(n, other_core) for n in near]
    pieces = near + other
    out, panel = first_product(
        pieces,
        [o0, o_back, o_ahead, q0, q_ahead, q_back],
        [(0, 0), (0, -1), (0, 1), (1, 0), (1, 1), (1, -1)],
    )
    out = rest_product(out, panel, [o_far], [(0, 2)])
    return rest_product(out, panel, [q_far], [(1, 2)])


def solution(mesh):
    fine = Mesh(mesh.devices.reshape(SIZES), AXES)
    return jax.shard_map(
        per_device,
        mesh=fine,
        in_specs=(P(None, None, AXES),),
        out_specs=P(None, ("zl", "core"), ("zh", "x", "y")),
        check_vma=False,
    )
```

```python
import functools
import itertools

import jax
import jax.numpy as jnp
from jax import lax
from jax.experimental import pallas as pl
from jax.experimental.pallas import tpu as pltpu
from jax.sharding import Mesh, PartitionSpec as P


AXES = ("zl", "core", "zh", "x", "y")
SIZES = (4, 2, 2, 4, 4)
NT = (((1,), (1,)), ((), ()))
STEPS = (0, -1, 1, 2)
VMEM = pl.BlockSpec(memory_space=pltpu.VMEM)
ANY = pl.BlockSpec(memory_space=pl.ANY)


def linear(place):
    index = 0
    for coordinate, size in zip(place, SIZES):
        index = index * size + coordinate
    return index


def permute(value, target):
    pairs = [(linear(p), linear(target(*p))) for p in itertools.product(*map(range, SIZES))]
    return lax.ppermute(value, AXES, pairs)


def first_shift(step):
    def target(zl, core, zh, x, y):
        return (zl, core, zh, (x + step) % 4, y) if core == 0 else (zl, core, zh, x, (y + step) % 4)

    return target


def second_shift(step):
    def target(zl, core, zh, x, y):
        return (zl, core, zh, x, (y + step) % 4) if core == 0 else (zl, core, zh, (x + step) % 4, y)

    return target


def across(zl, core, zh, x, y):
    return (zl, core, 1 - zh, x, y)


def to_panel(zl, core, zh, x, y):
    block = linear((zl, core, zh, x, y))
    column, slot = block // 8, block % 8
    return (slot % 4, slot // 4, column // 16, column // 4 % 4, column % 4)


def line_swap(bits):
    return lambda zl, core, zh, x, y: (zl ^ bits, core, zh, x, y)


def other_core(zl, core, zh, x, y):
    return (zl, 1 - core, zh, x, y)


def whiten_kernel(spectra, whitened):
    real = spectra[0].astype(jnp.float32)
    imag = spectra[1].astype(jnp.float32)
    factor = jnp.minimum(lax.rsqrt(real * real + imag * imag), 1.0)
    whitened[0] = (real * factor).astype(jnp.bfloat16)
    whitened[1] = (imag * factor).astype(jnp.bfloat16)


def line_kernel(*refs):
    *shares, line = refs
    for s, share in enumerate(shares):
        whiten_kernel(share, line.at[s])


def whiten(spectra):
    return pl.pallas_call(
        whiten_kernel,
        out_shape=jax.ShapeDtypeStruct(spectra.shape, jnp.bfloat16),
        compiler_params=pltpu.CompilerParams(vmem_limit_bytes=4 << 20),
        name="whiten",
    )(spectra)


def whitened_line(shares):
    return pl.pallas_call(
        line_kernel,
        in_specs=[VMEM] * len(shares),
        out_specs=VMEM,
        out_shape=jax.ShapeDtypeStruct((len(shares),) + shares[0].shape, shares[0].dtype),
        compiler_params=pltpu.CompilerParams(vmem_limit_bytes=4 << 20),
        name="line",
    )(*shares)


def row_of(width, line, s):
    _, core, zh, x, y = (lax.axis_index(a) for a in AXES)
    plane, second = line
    px = (x + jnp.where(core == 0, STEPS[s], second) + 4) % 4
    py = (y + jnp.where(core == 0, second, STEPS[s]) + 4) % 4
    return pl.multiple_of(((zh ^ plane) * 16 + px * 4 + py) * width, 16)


def multiply(scale, width, lines, groups, panel, out, tile, sem):
    pairs = [range(g, min(g + 2, len(groups))) for g in range(0, len(groups), 2)]

    def copies(n):
        return [
            pltpu.make_async_copy(
                tile.at[n % 2, :, pl.ds((k * 4 + s) * width, width)],
                out.at[:, pl.ds(row_of(width, lines[g], s), width)],
                sem.at[n % 2],
            )
            for k, g in enumerate(pairs[n])
            for s in range(4)
        ]

    def dot(a, b):
        return lax.dot_general(a, b, NT, preferred_element_type=jnp.float32)

    for n, pair in enumerate(pairs):
        rows = len(pair) * 4 * width
        parts = [jnp.concatenate([groups[g][:, k].reshape(4 * width, -1) for g in pair]) for k in range(2)]
        left = jnp.concatenate(parts, 1)
        if n >= 2:
            for copy in copies(n - 2):
                copy.wait()
        real = dot(left, jnp.concatenate([panel[0], panel[1]], 1))
        tile[n % 2, 0, :rows] = (real * scale).astype(jnp.bfloat16)
        imag = dot(left, jnp.concatenate([panel[2], panel[0]], 1))
        tile[n % 2, 1, :rows] = (imag * scale).astype(jnp.bfloat16)
        for copy in copies(n):
            copy.start()
    for n in range(max(len(pairs) - 2, 0), len(pairs)):
        for copy in copies(n):
            copy.wait()


def first_kernel(scale, width, lines, *refs):
    pieces, groups = refs[:8], refs[8:8 + len(lines)]
    out, panel, tile, sem = refs[-4:]
    zl, core = lax.axis_index("zl"), lax.axis_index("core")
    for s, piece in enumerate(pieces):
        slot = (core ^ (s // 4)) * 4 + (zl ^ (s % 4))
        at = pl.ds(pl.multiple_of(slot * width, 16), width)
        panel[0, at, :] = piece[0]
        panel[1, at, :] = piece[1]
        panel[2, at, :] = -piece[1]
    multiply(scale, width, lines, groups, panel, out, tile, sem)


def rest_kernel(scale, width, lines, panel, *refs):
    groups = refs[:len(lines)]
    out, tile, sem = refs[-3:]
    multiply(scale, width, lines, groups, panel, out, tile, sem)


def options(count, width, columns, segments):
    return dict(
        scratch_shapes=[
            pltpu.VMEM((2, 2, min(count, 2) * 4 * width, columns), jnp.bfloat16),
            pltpu.SemaphoreType.DMA((2,)),
        ],
        cost_estimate=pl.CostEstimate(
            flops=count * 32 * width * columns * segments, bytes_accessed=1 << 20, transcendentals=0
        ),
        compiler_params=pltpu.CompilerParams(vmem_limit_bytes=20 << 20),
    )


def first_product(pieces, groups, lines):
    count, (_, _, width, segments) = len(groups), groups[0].shape
    return pl.pallas_call(
        functools.partial(first_kernel, 1.0 / segments, width, lines),
        in_specs=[VMEM] * (8 + count),
        out_specs=[ANY, VMEM],
        out_shape=[
            jax.ShapeDtypeStruct((2, 32 * width, 8 * width), jnp.bfloat16),
            jax.ShapeDtypeStruct((3, 8 * width, segments), jnp.bfloat16),
        ],
        **options(count, width, 8 * width, segments),
    )(*pieces, *groups)


def rest_product(out, panel, groups, lines):
    count, (_, _, width, segments) = len(groups), groups[0].shape
    return pl.pallas_call(
        functools.partial(rest_kernel, 1.0 / segments, width, lines),
        in_specs=[VMEM] * (1 + count) + [ANY],
        out_specs=ANY,
        out_shape=jax.ShapeDtypeStruct(out.shape, jnp.bfloat16),
        input_output_aliases={1 + count: 0},
        **options(count, width, 8 * width, segments),
    )(panel, *groups, out)


def per_device(spectra):
    spectra = jnp.transpose(spectra, (0, 2, 1))
    piece = whiten(permute(spectra, to_panel))
    crossed = permute(spectra, across)

    def line(share):
        back = permute(share, first_shift(1))
        ahead = permute(share, first_shift(-1))
        far = permute(share, first_shift(2))
        return whitened_line([share, back, ahead, far])

    o0 = line(spectra)
    o_back = permute(o0, second_shift(1))
    o_ahead = permute(o0, second_shift(-1))
    o_far = permute(o_back, second_shift(1))
    q0 = line(crossed)
    q_back = permute(q0, second_shift(1))
    q_ahead = permute(q0, second_shift(-1))
    q_far = permute(q_ahead, second_shift(-1))

    near1 = permute(piece, line_swap(1))
    near2 = permute(piece, line_swap(2))
    near3 = permute(near2, line_swap(1))
    near = [piece, near1, near2, near3]
    other = [permute(n, other_core) for n in near]
    pieces = near + other
    out, panel = first_product(
        pieces,
        [o0, o_back, o_ahead, q0, q_ahead, q_back],
        [(0, 0), (0, -1), (0, 1), (1, 0), (1, 1), (1, -1)],
    )
    out = rest_product(out, panel, [o_far], [(0, 2)])
    return rest_product(out, panel, [q_far], [(1, 2)])


def solution(mesh):
    fine = Mesh(mesh.devices.reshape(SIZES), AXES)
    return jax.shard_map(
        per_device,
        mesh=fine,
        in_specs=(P(None, None, AXES),),
        out_specs=P(None, ("zl", "core"), ("zh", "x", "y")),
        check_vma=False,
    )
```
